32 devices in a mesh: gz: 4 (over y, x), gy: 8 (over z, core).
Axes of the slice: x: 2, y: 2, z: 4, core: 2. Of those that a mesh axis runs over, the one named last changes fastest.
Arguments:
- activations: bfloat16 [8, 128, 12288], P('gz', 'gy'), may hold values from -6 to 6
- grad_out: bfloat16 [8, 128, 12288], P('gz', 'gy'), may hold values from -6 to 6
- relu_mask: int32 [8, 128, 12288], P('gz', 'gy'), may hold values 0 or 1
- kernel: bfloat16 [3, 3, 3, 32, 32], replicated, may hold values from -0.21875 to 0.21875
- bias: float32 [32], replicated, may hold values from -3 to 3
Outputs:
- output: bfloat16 [8, 128, 12288], P('gz', 'gy')
- grad_input: bfloat16 [8, 128, 12288], P('gz', 'gy')
- grad_kernel: float32 [3, 3, 3, 32, 32], replicated
- grad_bias: float32 [32], replicated
The draws below stay inside these ranges and needn't reach their ends.
All inputs are finite; a program needn't handle non-finite values. No bound on the sum of `relu_mask` on one device may be relied on, other than what follows from the above.
Results may differ from the reference program's by a relative error of at most 0.001.
Values may be sent and summed in bfloat16 or wider, within the bound.
A program may use at most 192 MiB of HBM per device.

```python
import math
import jax
import jax.numpy as jnp
from jax import lax

C = 32
NX = 384
NZ = 8
NY = 128


def set_ends(result, stream_key, least, top_value):
    spot = [jax.random.randint(jax.random.fold_in(stream_key, axis), (), 0, length) for axis, length in enumerate(result.shape)]
    longest = result.shape.index(max(result.shape))
    beside = spot[:longest] + [(spot[longest] + 1) % result.shape[longest]] + spot[longest + 1:]
    return result.at[tuple(spot)].set(least).at[tuple(beside)].set(top_value)


def level_of(stream_key, shape, cuts, smallest, top_value):
    gain = 1.0
    for axis_at, parts in cuts:
        heights = jax.random.uniform(jax.random.fold_in(jax.random.fold_in(stream_key, 6), axis_at), (parts,), jnp.float32, smallest / len(cuts), top_value / len(cuts))
        gain = gain * jnp.repeat(jnp.exp(heights), shape[axis_at] // parts).reshape((-1,) + (1,) * (len(shape) - 1 - axis_at))
    return gain


def centred(stream_key, shape, spread, limit, shards=(), dtype=jnp.bfloat16):
    gain = level_of(stream_key, shape, shards, -0.22, 0.18) if shards else 1.0
    result = jax.random.normal(stream_key, shape, jnp.float32) * spread * gain
    return jnp.minimum(jnp.maximum(result, -limit), limit).astype(dtype)


def setup_inputs(seed: int = 0) -> dict:
    key_of = jax.random.split(jax.random.key(seed), 6)
    return {
        "activations": centred(key_of[0], (NZ, NY, NX * C), 1.0, 6.0, ((0, 4), (1, 8))),
        "grad_out": centred(key_of[1], (NZ, NY, NX * C), 1.0, 6.0, ((0, 4), (1, 8))),
        "relu_mask": set_ends((jax.random.randint(key_of[2], (NZ, NY, NX * C), 0, 2) < 1).astype(jnp.int32), jax.random.fold_in(key_of[2], 1), 0, 1),
        "kernel": centred(key_of[3], (3, 3, 3, C, C), (27 * C) ** -0.5, 0.21875),
        "bias": centred(key_of[4], (C,), 0.5, 3.0, (), jnp.float32),
    }


def convolve(volume, weights):
    return lax.conv_general_dilated(volume[None], weights, (1, 1, 1), [(1, 1), (1, 1), (1, 1)], dimension_numbers=('NDHWC', 'DHWIO', 'NDHWC'), precision=lax.Precision.HIGHEST)[0]

def reference(activations, grad_out, relu_mask, kernel, bias):
    inputs = activations.astype(jnp.float32).reshape(NZ, NY, NX, C)
    weights = kernel.astype(jnp.float32)
    preact, pullback = jax.vjp(convolve, inputs, weights)
    output = jnp.maximum(preact + bias, 0.0).astype(jnp.bfloat16).reshape(NZ, NY, NX * C)
    grad_pre = (grad_out * relu_mask.astype(jnp.bfloat16)).astype(jnp.float32).reshape(NZ, NY, NX, C)
    grad_input, grad_weights = pullback(grad_pre)
    scaling = 1.0 / math.sqrt(NZ * NY * NX)
    grad_kernel = grad_weights * scaling
    grad_bias = lax.optimization_barrier(jnp.sum(grad_pre, axis=(0, 1, 2))) * scaling
    return (output, grad_input.astype(jnp.bfloat16).reshape(NZ, NY, NX * C), grad_kernel, grad_bias)
```

```python
import functools
import math

import jax
import jax.numpy as jnp
from jax import lax
from jax.experimental import pallas as pl
from jax.experimental.pallas import tpu as pltpu
from jax.sharding import PartitionSpec as P

MESH = pl.DeviceIdType.MESH
BF = jnp.bfloat16
F32 = jnp.float32
WIN = 256
EDGE = 128


def iota(shape, dim):
    return lax.broadcasted_iota(jnp.int32, shape, dim)


def body(cfg, act, go, mask, kern, bias, out, gin, gker, gbias,
         sa, ea, sg, eg, wf, wb, k2, k2t, gp, gpt, za, zg, sta, stg, ya, yg,
         part, ra, pa, rb, pb, res,
         halo_send, halo_recv, a_send, a_recv, b_send, b_recv, c_send, c_recv):
    n_z, n_y, zc, yc, width, ch, rows, scaling = cfg
    planes = zc + 2
    vox = WIN // ch
    blocks = width // WIN
    half = blocks // 2
    hw = width // 2
    taps = 9
    iz = lax.axis_index("gz")
    iy = lax.axis_index("gy")

    has = {-1: lambda i, n: i > 0, 0: lambda i, n: i >= 0, 1: lambda i, n: i < n - 1}

    barrier = pltpu.get_barrier_semaphore()
    for k in range(1, n_y):
        pl.semaphore_signal(barrier, inc=1, device_id=(iz, lax.rem(iy + k, n_y)), device_id_type=MESH)
    for k in range(1, n_z):
        pl.semaphore_signal(barrier, inc=1, device_id=(lax.rem(iz + k, n_z), iy), device_id_type=MESH)
    for dz in (-1, 1):
        for dy in (-1, 1):
            @pl.when(has[dz](iz, n_z) & has[dy](iy, n_y))
            def _():
                pl.semaphore_signal(barrier, inc=1, device_id=(iz + dz, iy + dy), device_id_type=MESH)

    def stage(src, st):
        for z in range(zc):
            for side, row in ((0, yc - 1), (1, 0)):
                base = (row // 8) * 8
                for c in range(0, hw, 512):
                    lo = src[z, :, c:c + 512].astype(F32)[row:row + 1]
                    hi = src[z, :, hw + c:hw + c + 512].astype(F32)[row:row + 1]
                    st[side, z, :, c:c + 512] = jnp.concatenate([lo, hi], axis=0).astype(BF)

    def copies(src, st, zb, yb, which):
        found = []

        def add(dz, dy, src_ref, dst_ref):
            i = len(found)
            found.append((dz, dy, pltpu.make_async_remote_copy(
                src_ref=src_ref, dst_ref=dst_ref,
                send_sem=halo_send.at[which, i], recv_sem=halo_recv.at[which, i],
                device_id=(iz + dz, iy + dy), device_id_type=MESH)))

        add(1, 0, src.at[zc - 1], zb.at[0])
        add(-1, 0, src.at[0], zb.at[1])
        for side, dy in ((0, 1), (1, -1)):
            add(0, dy, st.at[side], yb.at[side, pl.ds(1, zc)])
            add(1, dy, st.at[side, zc - 1], yb.at[side, 0])
            add(-1, dy, st.at[side, 0], yb.at[side, planes - 1])
        return found

    def ok(dz, dy):
        return has[dz](iz, n_z) & has[dy](iy, n_y)

    def start(found):
        for dz, dy, copy in found:
            @pl.when(ok(dz, dy))
            def _():
                copy.start()

    def wait_recv(found):
        for dz, dy, copy in found:
            @pl.when(ok(-dz, -dy))
            def _():
                copy.wait_recv()

    def wait_send(found):
        for dz, dy, copy in found:
            @pl.when(ok(dz, dy))
            def _():
                copy.wait_send()

    def clear(found_dst):
        for dz, dy, ref in found_dst:
            @pl.when(jnp.logical_not(ok(-dz, -dy)))
            def _():
                ref[...] = jnp.zeros(ref.shape, BF)

    def targets(zb, yb):
        t = [(1, 0, zb.at[0]), (-1, 0, zb.at[1])]
        for side, dy in ((0, 1), (1, -1)):
            t.append((0, dy, yb.at[side, pl.ds(1, zc)]))
            t.append((1, dy, yb.at[side, 0]))
            t.append((-1, dy, yb.at[side, planes - 1]))
        return t

    stage(act, sta)
    clear(targets(za, ya))
    clear(targets(zg, yg))
    diag = sum(ok(dz, dy).astype(jnp.int32) for dz in (-1, 1) for dy in (-1, 1))
    pl.semaphore_wait(barrier, n_y - 1 + n_z - 1 + diag)

    act_copies = copies(act, sta, za, ya, 0)
    start(act_copies)

    def gp_step(j, total):
        lanes = pl.ds(pl.multiple_of(j * WIN, WIN), WIN)
        for z in range(zc):
            g = go[z, :, lanes] * mask[z, :, lanes].astype(F32).astype(BF)
            gp[z, :, lanes] = g
            sg[1, j + 1, z + 1] = g
            total = total + jnp.sum(g.astype(F32), axis=0, keepdims=True)
        return total

    bias_total = lax.fori_loop(0, blocks, gp_step, jnp.zeros((1, WIN), F32))
    stage(gp, stg)
    gp_copies = copies(gp, stg, zg, yg, 1)
    start(gp_copies)

    spread = (iota((ch, WIN), 1) % ch == iota((ch, WIN), 0)).astype(BF)
    k2[...] = jnp.dot(kern[...], spread, preferred_element_type=F32)

    def k2t_step(t, c):
        at = pl.ds(pl.multiple_of(t * ch, ch), ch)
        k2t[at, :] = lax.dot_general(kern[at, :], spread, (((0,), (0,)), ((), ())), preferred_element_type=F32)
        return c

    lax.fori_loop(0, 27, k2t_step, 0)
    lane_vox = iota((ch, WIN), 1) // ch

    def weights(w, t, get):
        blk = [get(e) for e in range(3)]
        for u in range(vox):
            m = jnp.zeros((ch, WIN), F32)
            for e in range(3):
                m = jnp.where(lane_vox == u - e + 1, blk[e], m)
            w[pl.ds(pl.multiple_of(t * WIN + u * ch, ch), ch), :] = m.astype(BF)
        base = taps * WIN
        zero = jnp.zeros((ch, WIN), F32)
        rows_of = [jnp.where(lane_vox == vox - 1, blk[2], zero)] + [zero] * (EDGE // ch - 2) + [jnp.where(lane_vox == 0, blk[0], zero)]
        for r, m in enumerate(rows_of):
            w[pl.ds(pl.multiple_of(base + t * EDGE + r * ch, ch), ch), :] = m.astype(BF)

    def weight_step(t, c):
        weights(wf, t, lambda e: k2[pl.ds(pl.multiple_of((t * 3 + e) * ch, ch), ch), :])
        weights(wb, t, lambda e: k2t[pl.ds(pl.multiple_of(((8 - t) * 3 + 2 - e) * ch, ch), ch), :])
        return c

    lax.fori_loop(0, taps, weight_step, 0)

    per = zc * yc
    gpt[...] = sg[1, 1:blocks + 1, 1:zc + 1].reshape(blocks * per, WIN).T

    row_id = iota((yc, WIN), 0)
    edge_low = iota((yc, EDGE), 1) < EDGE // 2

    def build(local, zb, yb, s, e):
        for b in range(3):
            s[b, 0] = jnp.zeros((planes, yc, WIN), BF)
            s[b, blocks + 1] = jnp.zeros((planes, yc, WIN), BF)
        for h in range(2):
            def step(jj, c):
                lanes = pl.ds(pl.multiple_of((h * half + jj) * WIN, WIN), WIN)
                near = pl.ds(pl.multiple_of(jj * WIN, WIN), WIN)
                j = h * half + jj + 1
                for p in range(planes):
                    raw = zb[0, :, lanes] if p == 0 else zb[1, :, lanes] if p == planes - 1 else local[p - 1, :, lanes]
                    x = raw.astype(F32)
                    low = yb[0, p, :, near].astype(F32)[h:h + 1]
                    high = yb[1, p, :, near].astype(F32)[h:h + 1]
                    s[1, j, p] = raw
                    s[0, j, p] = jnp.where(row_id == 0, low, pltpu.roll(x, 1, 0)).astype(BF)
                    s[2, j, p] = jnp.where(row_id == yc - 1, high, pltpu.roll(x, yc - 1, 0)).astype(BF)
                return c
            lax.fori_loop(0, half, step, 0)

        def edges(j, c):
            for b in range(3):
                for p in range(planes):
                    e[b, j, p] = jnp.where(edge_low, s[b, j + 2, p, :, :EDGE], s[b, j, p, :, WIN - EDGE:])
            return c
        lax.fori_loop(0, blocks, edges, 0)

    group = blocks // 3
    m_rows = group * per

    def conv(s, e, w, dst, finish):
        def step(g, c):
            j0 = g * group
            pieces = []
            for a in range(3):
                for b in range(3):
                    pieces.append(s[b, pl.ds(j0 + 1, group), a:a + zc].reshape(m_rows, WIN))
            for a in range(3):
                for b in range(3):
                    pieces.append(e[b, pl.ds(j0, group), a:a + zc].reshape(m_rows, EDGE))
            acc = jnp.dot(jnp.concatenate(pieces, axis=1), w[...], preferred_element_type=F32)
            acc = finish(acc).astype(BF).reshape(group, zc, yc, WIN)
            for q in range(group):
                dst[:, :, pl.ds(pl.multiple_of((j0 + q) * WIN, WIN), WIN)] = acc[q]
            return c
        lax.fori_loop(0, blocks // group, step, 0)

    wait_recv(act_copies)
    build(act, za, ya, sa, ea)

    q_vox = iota((WIN, WIN), 0) // ch
    p_vox = iota((WIN, WIN), 1) // ch
    grp = iota((ch, EDGE), 1) // ch

    def fold_lanes(x):
        y = x[:, :EDGE] + x[:, EDGE:] if x.shape[1] == WIN else x
        y = y + pltpu.roll(y, 64, 1)
        return y + pltpu.roll(y, 32, 1)

    def fold_rows(x):
        y = x[:ch]
        for v in range(1, vox):
            y = y + x[v * ch:(v + 1) * ch]
        return y

    def tap_step(t, c):
        a = t // 3
        b = lax.rem(t, 3)
        rhs = sa[b, 1:blocks + 1, pl.ds(a, zc)].reshape(blocks * per, WIN)
        edge = ea[b, :, pl.ds(a, zc)].reshape(blocks * per, EDGE)
        d = jnp.dot(gpt[...], rhs, preferred_element_type=F32)
        de = jnp.dot(gpt[...], edge, preferred_element_type=F32)
        total = jnp.zeros((ch, EDGE), F32)
        for k in range(3):
            one = fold_lanes(fold_rows(jnp.where(p_vox - q_vox + 1 == k, d, 0.0)))
            if k == 0:
                one = one + fold_lanes(jnp.where(grp == EDGE // ch - 1, de[:ch], 0.0))
            if k == 2:
                one = one + fold_lanes(jnp.where(grp == 0, de[WIN - ch:], 0.0))
            total = jnp.where(grp == k, one, total)
        part[pl.ds(pl.multiple_of(t * ch, ch), ch), :] = total
        return c

    lax.fori_loop(0, taps, tap_step, 0)
    tail = part.shape[0] - taps * ch
    bias_row = fold_lanes(jnp.broadcast_to(bias_total, (8, WIN)))
    part[taps * ch:taps * ch + 8, :] = bias_row
    if tail > 8:
        part[taps * ch + 8:, :] = jnp.zeros((tail - 8, EDGE), F32)

    a_copies = []
    for k in range(1, n_y):
        to = lax.rem(iy + k, n_y)
        a_copies.append(pltpu.make_async_remote_copy(
            src_ref=part.at[pl.ds(pl.multiple_of(to * rows, 8), rows)], dst_ref=ra.at[k],
            send_sem=a_send.at[k], recv_sem=a_recv.at[k], device_id=(iz, to), device_id_type=MESH))
        a_copies[-1].start()

    bias_row8 = jnp.concatenate([bias[...]] * vox, axis=1)
    conv(sa, ea, wf, out, lambda acc: jnp.maximum(acc + bias_row8, 0.0))

    total = part[pl.ds(pl.multiple_of(iy * rows, 8), rows), :]
    for k, copy in enumerate(a_copies):
        copy.wait_recv()
        total = total + ra[k + 1]
    pa[...] = total
    b_copies = []
    for k in range(1, n_z):
        b_copies.append(pltpu.make_async_remote_copy(
            src_ref=pa, dst_ref=rb.at[iz],
            send_sem=b_send.at[k], recv_sem=b_recv.at[k],
            device_id=(lax.rem(iz + k, n_z), iy), device_id_type=MESH))
        b_copies[-1].start()

    wait_recv(gp_copies)
    build(gp, zg, yg, sg, eg)

    rb[pl.ds(iz, 1)] = total[None]
    for copy in b_copies:
        copy.wait_recv()
    total = rb[0]
    for k in range(1, n_z):
        total = total + rb[k]
    pb[...] = total
    mine = pl.ds(pl.multiple_of(iy * rows, 8), rows)
    c_copies = []
    for k in range(1, n_y):
        c_copies.append(pltpu.make_async_remote_copy(
            src_ref=pb, dst_ref=res.at[mine],
            send_sem=c_send.at[k], recv_sem=c_recv.at[k],
            device_id=(iz, lax.rem(iy + k, n_y)), device_id_type=MESH))
        c_copies[-1].start()
    res[mine, :] = total

    conv(sg, eg, wb, gin, lambda acc: acc)

    for copy in c_copies:
        copy.wait_recv()
    for t in range(taps):
        turned = (res[t * ch:(t + 1) * ch, :] * scaling).T
        gker[t * 3 * ch:(t + 1) * 3 * ch, :] = turned[:3 * ch]
    gbias[...] = res[taps * ch:taps * ch + 8, :][0:1, :ch] * scaling

    wait_send(act_copies)
    wait_send(gp_copies)
    for copy in a_copies + b_copies + c_copies:
        copy.wait_send()


def local(n_z, n_y, activations, grad_out, relu_mask, kernel, bias):
    zc, yc, width = activations.shape
    ch = kernel.shape[-1]
    blocks = width // WIN
    planes = zc + 2
    voxels = zc * n_z * yc * n_y * (width // ch)
    rows = -(-(9 * ch + 8) // (n_y * 8)) * 8
    cfg = (n_z, n_y, zc, yc, width, ch, rows, 1.0 / math.sqrt(voxels))
    vmem = pl.BlockSpec(memory_space=pltpu.VMEM)
    dma = pltpu.SemaphoreType.DMA
    s_shape = pltpu.VMEM((3, blocks + 2, planes, yc, WIN), BF)
    e_shape = pltpu.VMEM((3, blocks, planes, yc, EDGE), BF)
    w_shape = pltpu.VMEM((9 * (WIN + EDGE), WIN), BF)
    k_shape = pltpu.VMEM((27 * ch, WIN), F32)
    stage_shape = pltpu.VMEM((2, zc, 2, width // 2), BF)
    rim_shape = pltpu.VMEM((2, planes, 2, width // 2), BF)
    plane_shape = pltpu.VMEM((2, yc, width), BF)
    output, grad_input, grad_kernel, grad_bias = pl.pallas_call(
        functools.partial(body, cfg),
        out_shape=(
            jax.ShapeDtypeStruct(activations.shape, BF),
            jax.ShapeDtypeStruct(activations.shape, BF),
            jax.ShapeDtypeStruct((27 * ch, ch), F32),
            jax.ShapeDtypeStruct((1, ch), F32),
        ),
        in_specs=[vmem] * 5,
        out_specs=(vmem,) * 4,
        scratch_shapes=[
            s_shape, e_shape, s_shape, e_shape, w_shape, w_shape, k_shape, k_shape,
            pltpu.VMEM((zc, yc, width), BF),
            pltpu.VMEM((WIN, blocks * zc * yc), BF),
            plane_shape, plane_shape, stage_shape, stage_shape, rim_shape, rim_shape,
            pltpu.VMEM((n_y * rows, EDGE), F32),
            pltpu.VMEM((n_y, rows, EDGE), F32),
            pltpu.VMEM((rows, EDGE), F32),
            pltpu.VMEM((n_z, rows, EDGE), F32),
            pltpu.VMEM((rows, EDGE), F32),
            pltpu.VMEM((n_y * rows, EDGE), F32),
            dma((2, 8)), dma((2, 8)),
            dma((n_y,)), dma((n_y,)), dma((n_z,)), dma((n_z,)), dma((n_y,)), dma((n_y,)),
        ],
        compiler_params=pltpu.CompilerParams(
            collective_id=0, has_side_effects=True, vmem_limit_bytes=60000 * 1024
        ),
    )(activations, grad_out, relu_mask, kernel.reshape(27 * ch, ch), bias.reshape(1, ch))
    return output, grad_input, grad_kernel.reshape(kernel.shape), grad_bias.reshape(ch)


def solution(mesh):
    placed = (P("gz", "gy", None), P("gz", "gy", None), P("gz", "gy", None), P(), P())
    return jax.shard_map(
        functools.partial(local, mesh.shape["gz"], mesh.shape["gy"]),
        mesh=mesh,
        in_specs=placed,
        out_specs=(P("gz", "gy", None), P("gz", "gy", None), P(), P()),
        check_vma=False,
    )
```

```python
import functools
import math

import jax
import jax.numpy as jnp
from jax import lax
from jax.experimental import pallas as pl
from jax.experimental.pallas import tpu as pltpu
from jax.sharding import PartitionSpec as P

MESH = pl.DeviceIdType.MESH
BF = jnp.bfloat16
F32 = jnp.float32
WIN = 256
EDGE = 128


def iota(shape, dim):
    return lax.broadcasted_iota(jnp.int32, shape, dim)


def body(cfg, act, go, mask, kern, bias, out, gin, gker, gbias,
         sa, ea, sg, eg, wf, wb, k2, k2t, gp, gpt, za, zg, sta, stg, ya, yg,
         part, ra, pa, rb, pb, res, rly,
         halo_send, halo_recv, a_send, a_recv, b_send, b_recv, c_send, c_recv):
    n_z, n_y, zc, yc, width, ch, rows, scaling = cfg
    planes = zc + 2
    vox = WIN // ch
    blocks = width // WIN
    half = blocks // 2
    hw = width // 2
    taps = 9
    iz = lax.axis_index("gz")
    iy = lax.axis_index("gy")

    has = {-1: lambda i, n: i > 0, 0: lambda i, n: i >= 0, 1: lambda i, n: i < n - 1}

    barrier = pltpu.get_barrier_semaphore()
    for k in range(1, n_y):
        pl.semaphore_signal(barrier, inc=1, device_id=(iz, lax.rem(iy + k, n_y)), device_id_type=MESH)
    for k in range(1, n_z):
        pl.semaphore_signal(barrier, inc=1, device_id=(lax.rem(iz + k, n_z), iy), device_id_type=MESH)
    for dz in (-1, 1):
        for dy in (-1, 1):
            @pl.when(has[dz](iz, n_z) & has[dy](iy, n_y))
            def _():
                pl.semaphore_signal(barrier, inc=1, device_id=(iz + dz, iy + dy), device_id_type=MESH)

    def stage(src, st):
        for z in range(zc):
            for side, row in ((0, yc - 1), (1, 0)):
                base = (row // 8) * 8
                for c in range(0, hw, 512):
                    lo = src[z, :, c:c + 512].astype(F32)[row:row + 1]
                    hi = src[z, :, hw + c:hw + c + 512].astype(F32)[row:row + 1]
                    st[side, z, :, c:c + 512] = jnp.concatenate([lo, hi], axis=0).astype(BF)

    even = 1 - lax.rem(iz, 2)
    s = 2 * even - 1
    pair_plane = (zc - 1) * even
    cross_plane = zc - 1 - pair_plane
    crosses = (iz - s >= 0) & (iz - s < n_z)
    relays = (iz + 2 * s >= 0) & (iz + 2 * s < n_z)

    def ok(dz, dy):
        return has[dz](iz, n_z) & has[dy](iy, n_y)

    def copies(src, st, zb, yb, which):
        found = []
        low, high = pl.ds(0, hw), pl.ds(hw, hw)

        def add(sends, gets, to, src_ref, dst_ref):
            i = len(found)
            found.append((sends, gets, pltpu.make_async_remote_copy(
                src_ref=src_ref, dst_ref=dst_ref,
                send_sem=halo_send.at[which, i], recv_sem=halo_recv.at[which, i],
                device_id=to, device_id_type=MESH)))

        add(None, None, (iz + s, iy), src.at[pair_plane], zb.at[1 - even])
        add(crosses, relays, (iz + s, iy), src.at[cross_plane, :, low], rly.at[which, 0])
        add(crosses, relays, (iz - 2 * s, iy), src.at[cross_plane, :, high], rly.at[which, 1])
        add(relays, crosses, (iz + 2 * s, iy), rly.at[which, 0], zb.at[1 - even, :, low])
        add(relays, crosses, (iz + s, iy), rly.at[which, 1], zb.at[even, :, high])
        for side, dy in ((0, 1), (1, -1)):
            add(ok(0, dy), ok(0, -dy), (iz, iy + dy), st.at[side], yb.at[side, pl.ds(1, zc)])
        for side, dy in ((0, 1), (1, -1)):
            add(ok(1, dy), ok(-1, -dy), (iz + 1, iy + dy), st.at[side, zc - 1], yb.at[side, 0])
            add(ok(-1, dy), ok(1, -dy), (iz - 1, iy + dy), st.at[side, 0], yb.at[side, planes - 1])
        return found

    def guarded(condition, action):
        if condition is None:
            action()
        else:
            pl.when(condition)(action)

    def start(found, picks):
        for i in picks:
            guarded(found[i][0], found[i][2].start)

    def wait_recv(found, picks):
        for i in picks:
            guarded(found[i][1], found[i][2].wait_recv)

    def wait_send(found):
        for sends, _, copy in found:
            guarded(sends, copy.wait_send)

    HOP, PAIR, FORWARD_LOW, FORWARD_HIGH = (1, 2), (0,), (3,), (4,)
    SIDES, CORNERS = (5, 6), (7, 8, 9, 10)

    def clear(zb, yb):
        def one(ref):
            ref[...] = jnp.zeros(ref.shape, BF)

        pl.when(jnp.logical_not(crosses))(lambda: one(zb.at[1 - even]))
        for side, dy in ((0, 1), (1, -1)):
            for dz, ref in ((0, yb.at[side, pl.ds(1, zc)]), (1, yb.at[side, 0]), (-1, yb.at[side, planes - 1])):
                pl.when(jnp.logical_not(ok(-dz, -dy)))(functools.partial(one, ref))

    stage(act, sta)
    clear(za, ya)
    clear(zg, yg)
    diag = sum(ok(dz, dy).astype(jnp.int32) for dz in (-1, 1) for dy in (-1, 1))
    pl.semaphore_wait(barrier, n_y - 1 + n_z - 1 + diag)

    act_copies = copies(act, sta, za, ya, 0)
    start(act_copies, SIDES + HOP + PAIR + CORNERS)

    def gp_step(j, total):
        lanes = pl.ds(pl.multiple_of(j * WIN, WIN), WIN)
        for z in range(zc):
            g = go[z, :, lanes] * mask[z, :, lanes].astype(F32).astype(BF)
            gp[z, :, lanes] = g
            sg[1, j + 1, z + 1] = g
            total = total + jnp.sum(g.astype(F32), axis=0, keepdims=True)
        return total

    bias_total = lax.fori_loop(0, blocks, gp_step, jnp.zeros((1, WIN), F32))
    stage(gp, stg)
    gp_copies = copies(gp, stg, zg, yg, 1)
    wait_recv(act_copies, HOP)
    start(act_copies, FORWARD_LOW + FORWARD_HIGH)
    start(gp_copies, SIDES + HOP + PAIR + CORNERS)

    spread = (iota((ch, WIN), 1) % ch == iota((ch, WIN), 0)).astype(BF)
    k2[...] = jnp.dot(kern[...], spread, preferred_element_type=F32)

    def k2t_step(t, c):
        at = pl.ds(pl.multiple_of(t * ch, ch), ch)
        k2t[at, :] = lax.dot_general(kern[at, :], spread, (((0,), (0,)), ((), ())), preferred_element_type=F32)
        return c

    lax.fori_loop(0, 27, k2t_step, 0)
    lane_vox = iota((ch, WIN), 1) // ch

    def weights(w, t, get):
        blk = [get(e) for e in range(3)]
        for u in range(vox):
            m = jnp.zeros((ch, WIN), F32)
            for e in range(3):
                m = jnp.where(lane_vox == u - e + 1, blk[e], m)
            w[pl.ds(pl.multiple_of(t * WIN + u * ch, ch), ch), :] = m.astype(BF)
        base = taps * WIN
        zero = jnp.zeros((ch, WIN), F32)
        rows_of = [jnp.where(lane_vox == vox - 1, blk[2], zero)] + [zero] * (EDGE // ch - 2) + [jnp.where(lane_vox == 0, blk[0], zero)]
        for r, m in enumerate(rows_of):
            w[pl.ds(pl.multiple_of(base + t * EDGE + r * ch, ch), ch), :] = m.astype(BF)

    def weight_step(t, c):
        weights(wf, t, lambda e: k2[pl.ds(pl.multiple_of((t * 3 + e) * ch, ch), ch), :])
        weights(wb, t, lambda e: k2t[pl.ds(pl.multiple_of(((8 - t) * 3 + 2 - e) * ch, ch), ch), :])
        return c

    lax.fori_loop(0, taps, weight_step, 0)

    per = zc * yc
    for z in range(zc):
        gpt[z] = sg[1, 1:blocks + 1, z + 1].reshape(blocks * yc, WIN).T

    row_id = iota((yc, WIN), 0)
    edge_low = iota((yc, EDGE), 1) < EDGE // 2

    def pad(s):
        for b in range(3):
            s[b, 0] = jnp.zeros((planes, yc, WIN), BF)
            s[b, blocks + 1] = jnp.zeros((planes, yc, WIN), BF)

    def build(local, zb, yb, s, e, which):
        for h in range(2):
            def step(jj, c):
                lanes = pl.ds(pl.multiple_of((h * half + jj) * WIN, WIN), WIN)
                near = pl.ds(pl.multiple_of(jj * WIN, WIN), WIN)
                j = h * half + jj + 1
                for p in which:
                    raw = zb[0, :, lanes] if p == 0 else zb[1, :, lanes] if p == planes - 1 else local[p - 1, :, lanes]
                    x = raw.astype(F32)
                    low = yb[0, p, :, near].astype(F32)[h:h + 1]
                    high = yb[1, p, :, near].astype(F32)[h:h + 1]
                    s[1, j, p] = raw
                    s[0, j, p] = jnp.where(row_id == 0, low, pltpu.roll(x, 1, 0)).astype(BF)
                    s[2, j, p] = jnp.where(row_id == yc - 1, high, pltpu.roll(x, yc - 1, 0)).astype(BF)
                return c
            lax.fori_loop(0, half, step, 0)

        def edges(j, c):
            for b in range(3):
                for p in which:
                    e[b, j, p] = jnp.where(edge_low, s[b, j + 2, p, :, :EDGE], s[b, j, p, :, WIN - EDGE:])
            return c
        lax.fori_loop(0, blocks, edges, 0)

    group = blocks // 3
    m_rows = group * per

    def conv(s, e, w, dst, finish):
        def step(g, c):
            j0 = g * group
            pieces = []
            for a in range(3):
                for b in range(3):
                    pieces.append(s[b, pl.ds(j0 + 1, group), a:a + zc].reshape(m_rows, WIN))
            for a in range(3):
                for b in range(3):
                    pieces.append(e[b, pl.ds(j0, group), a:a + zc].reshape(m_rows, EDGE))
            acc = jnp.dot(jnp.concatenate(pieces, axis=1), w[...], preferred_element_type=F32)
            acc = finish(acc).astype(BF).reshape(group, zc, yc, WIN)
            for q in range(group):
                dst[:, :, pl.ds(pl.multiple_of((j0 + q) * WIN, WIN), WIN)] = acc[q]
            return c
        lax.fori_loop(0, blocks // group, step, 0)

    inner, rim = tuple(range(1, zc + 1)), (0, planes - 1)
    pad(sa)
    pad(sg)
    wait_recv(act_copies, SIDES)
    build(act, za, ya, sa, ea, inner)

    q_vox = iota((WIN, WIN), 0) // ch
    p_vox = iota((WIN, WIN), 1) // ch
    grp = iota((ch, EDGE), 1) // ch

    def fold_lanes(x):
        y = x[:, :EDGE] + x[:, EDGE:] if x.shape[1] == WIN else x
        y = y + pltpu.roll(y, 64, 1)
        return y + pltpu.roll(y, 32, 1)

    def fold_rows(x):
        y = x[:ch]
        for v in range(1, vox):
            y = y + x[v * ch:(v + 1) * ch]
        return y

    def tap(a, b, zs, first):
        t = a * 3 + b
        d, de = None, None
        for z in zs:
            rhs = sa[b, 1:blocks + 1, a + z].reshape(blocks * yc, WIN)
            edge = ea[b, :, a + z].reshape(blocks * yc, EDGE)
            d1 = jnp.dot(gpt[z], rhs, preferred_element_type=F32)
            de1 = jnp.dot(gpt[z], edge, preferred_element_type=F32)
            d, de = (d1, de1) if d is None else (d + d1, de + de1)
        total = jnp.zeros((ch, EDGE), F32)
        for k in range(3):
            one = fold_lanes(fold_rows(jnp.where(p_vox - q_vox + 1 == k, d, 0.0)))
            if k == 0:
                one = one + fold_lanes(jnp.where(grp == EDGE // ch - 1, de[:ch], 0.0))
            if k == 2:
                one = one + fold_lanes(jnp.where(grp == 0, de[WIN - ch:], 0.0))
            total = jnp.where(grp == k, one, total)
        at = pl.ds(pl.multiple_of(t * ch, ch), ch)
        part[at, :] = total if first else part[at, :] + total

    def tap_loop(a, zs, first):
        def step(b, c):
            tap(a, b, zs, first)
            return c
        lax.fori_loop(0, 3, step, 0)

    for a in range(3):
        tap_loop(a, [z for z in range(zc) if a + z in inner], True)
    wait_recv(act_copies, PAIR + FORWARD_LOW + FORWARD_HIGH + CORNERS)
    wait_recv(gp_copies, HOP[1:])
    start(gp_copies, FORWARD_HIGH)
    build(act, za, ya, sa, ea, rim)
    wait_recv(gp_copies, HOP[:1])
    start(gp_copies, FORWARD_LOW)
    for a in (0, 2):
        tap_loop(a, [z for z in range(zc) if a + z in rim], False)
    tail = part.shape[0] - taps * ch
    bias_row = fold_lanes(jnp.broadcast_to(bias_total, (8, WIN)))
    part[taps * ch:taps * ch + 8, :] = bias_row
    if tail > 8:
        part[taps * ch + 8:, :] = jnp.zeros((tail - 8, EDGE), F32)

    a_copies = []
    for k in range(1, n_y):
        to = lax.rem(iy + k, n_y)
        a_copies.append(pltpu.make_async_remote_copy(
            src_ref=part.at[pl.ds(pl.multiple_of(to * rows, 8), rows)], dst_ref=ra.at[k],
            send_sem=a_send.at[k], recv_sem=a_recv.at[k], device_id=(iz, to), device_id_type=MESH))
        a_copies[-1].start()

    bias_row8 = jnp.concatenate([bias[...]] * vox, axis=1)
    conv(sa, ea, wf, out, lambda acc: jnp.maximum(acc + bias_row8, 0.0))

    total = part[pl.ds(pl.multiple_of(iy * rows, 8), rows), :]
    for k, copy in enumerate(a_copies):
        copy.wait_recv()
        total = total + ra[k + 1]
    pa[...] = total
    b_copies = []
    for k in range(1, n_z):
        b_copies.append(pltpu.make_async_remote_copy(
            src_ref=pa, dst_ref=rb.at[iz],
            send_sem=b_send.at[k], recv_sem=b_recv.at[k],
            device_id=(lax.rem(iz + k, n_z), iy), device_id_type=MESH))
        b_copies[-1].start()

    wait_recv(gp_copies, SIDES)
    build(gp, zg, yg, sg, eg, inner)

    rb[pl.ds(iz, 1)] = total[None]
    for copy in b_copies:
        copy.wait_recv()
    total = rb[0]
    for k in range(1, n_z):
        total = total + rb[k]
    pb[...] = total
    mine = pl.ds(pl.multiple_of(iy * rows, 8), rows)
    c_copies = []
    for k in range(1, n_y):
        c_copies.append(pltpu.make_async_remote_copy(
            src_ref=pb, dst_ref=res.at[mine],
            send_sem=c_send.at[k], recv_sem=c_recv.at[k],
            device_id=(iz, lax.rem(iy + k, n_y)), device_id_type=MESH))
        c_copies[-1].start()
    res[mine, :] = total

    wait_recv(gp_copies, PAIR + FORWARD_LOW + FORWARD_HIGH + CORNERS)
    build(gp, zg, yg, sg, eg, rim)
    conv(sg, eg, wb, gin, lambda acc: acc)

    for copy in c_copies:
        copy.wait_recv()
    for t in range(taps):
        turned = (res[t * ch:(t + 1) * ch, :] * scaling).T
        gker[t * 3 * ch:(t + 1) * 3 * ch, :] = turned[:3 * ch]
    gbias[...] = res[taps * ch:taps * ch + 8, :][0:1, :ch] * scaling

    wait_send(act_copies)
    wait_send(gp_copies)
    for copy in a_copies + b_copies + c_copies:
        copy.wait_send()


def local(n_z, n_y, activations, grad_out, relu_mask, kernel, bias):
    zc, yc, width = activations.shape
    ch = kernel.shape[-1]
    blocks = width // WIN
    planes = zc + 2
    voxels = zc * n_z * yc * n_y * (width // ch)
    rows = -(-(9 * ch + 8) // (n_y * 8)) * 8
    cfg = (n_z, n_y, zc, yc, width, ch, rows, 1.0 / math.sqrt(voxels))
    vmem = pl.BlockSpec(memory_space=pltpu.VMEM)
    dma = pltpu.SemaphoreType.DMA
    s_shape = pltpu.VMEM((3, blocks + 2, planes, yc, WIN), BF)
    e_shape = pltpu.VMEM((3, blocks, planes, yc, EDGE), BF)
    w_shape = pltpu.VMEM((9 * (WIN + EDGE), WIN), BF)
    k_shape = pltpu.VMEM((27 * ch, WIN), F32)
    stage_shape = pltpu.VMEM((2, zc, 2, width // 2), BF)
    rim_shape = pltpu.VMEM((2, planes, 2, width // 2), BF)
    plane_shape = pltpu.VMEM((2, yc, width), BF)
    output, grad_input, grad_kernel, grad_bias = pl.pallas_call(
        functools.partial(body, cfg),
        out_shape=(
            jax.ShapeDtypeStruct(activations.shape, BF),
            jax.ShapeDtypeStruct(activations.shape, BF),
            jax.ShapeDtypeStruct((27 * ch, ch), F32),
            jax.ShapeDtypeStruct((1, ch), F32),
        ),
        in_specs=[vmem] * 5,
        out_specs=(vmem,) * 4,
        scratch_shapes=[
            s_shape, e_shape, s_shape, e_shape, w_shape, w_shape, k_shape, k_shape,
            pltpu.VMEM((zc, yc, width), BF),
            pltpu.VMEM((zc, WIN, blocks * yc), BF),
            plane_shape, plane_shape, stage_shape, stage_shape, rim_shape, rim_shape,
            pltpu.VMEM((n_y * rows, EDGE), F32),
            pltpu.VMEM((n_y, rows, EDGE), F32),
            pltpu.VMEM((rows, EDGE), F32),
            pltpu.VMEM((n_z, rows, EDGE), F32),
            pltpu.VMEM((rows, EDGE), F32),
            pltpu.VMEM((n_y * rows, EDGE), F32),
            pltpu.VMEM((2, 2, yc, width // 2), BF),
            dma((2, 11)), dma((2, 11)),
            dma((n_y,)), dma((n_y,)), dma((n_z,)), dma((n_z,)), dma((n_y,)), dma((n_y,)),
        ],
        compiler_params=pltpu.CompilerParams(
            collective_id=0, has_side_effects=True, vmem_limit_bytes=60000 * 1024
        ),
    )(activations, grad_out, relu_mask, kernel.reshape(27 * ch, ch), bias.reshape(1, ch))
    return output, grad_input, grad_kernel.reshape(kernel.shape), grad_bias.reshape(ch)


def solution(mesh):
    placed = (P("gz", "gy", None), P("gz", "gy", None), P("gz", "gy", None), P(), P())
    return jax.shard_map(
        functools.partial(local, mesh.shape["gz"], mesh.shape["gy"]),
        mesh=mesh,
        in_specs=placed,
        out_specs=(P("gz", "gy", None), P("gz", "gy", None), P(), P()),
        check_vma=False,
    )
```

```python
import functools
import math

import jax
import jax.numpy as jnp
from jax import lax
from jax.experimental import pallas as pl
from jax.experimental.pallas import tpu as pltpu
from jax.sharding import PartitionSpec as P

MESH = pl.DeviceIdType.MESH
BF = jnp.bfloat16
F32 = jnp.float32
WIN = 256
EDGE = 128


def iota(shape, dim):
    return lax.broadcasted_iota(jnp.int32, shape, dim)


def body(cfg, act, go_far, mask_far, kern, bias, out, gin, gker, gbias,
         sa, ea, sg, eg, wf, wb, k2, k2t, gp, gpt, za, zg, sta, stg, ya, yg,
         part, ra, pa, rb, pb, res, rly, go, mask, load_sem,
         halo_send, halo_recv, a_send, a_recv, b_send, b_recv, c_send, c_recv):
    n_z, n_y, zc, yc, width, ch, rows, scaling = cfg
    planes = zc + 2
    vox = WIN // ch
    blocks = width // WIN
    half = blocks // 2
    hw = width // 2
    taps = 9
    iz = lax.axis_index("gz")
    iy = lax.axis_index("gy")

    has = {-1: lambda i, n: i > 0, 0: lambda i, n: i >= 0, 1: lambda i, n: i < n - 1}

    loads = [pltpu.make_async_copy(go_far, go, load_sem.at[0]), pltpu.make_async_copy(mask_far, mask, load_sem.at[1])]
    for load in loads:
        load.start()

    barrier = pltpu.get_barrier_semaphore()
    for k in range(1, n_y):
        pl.semaphore_signal(barrier, inc=1, device_id=(iz, lax.rem(iy + k, n_y)), device_id_type=MESH)
    for k in range(1, n_z):
        pl.semaphore_signal(barrier, inc=1, device_id=(lax.rem(iz + k, n_z), iy), device_id_type=MESH)
    for dz in (-1, 1):
        for dy in (-1, 1):
            @pl.when(has[dz](iz, n_z) & has[dy](iy, n_y))
            def _():
                pl.semaphore_signal(barrier, inc=1, device_id=(iz + dz, iy + dy), device_id_type=MESH)

    def stage(src, st):
        for z in range(zc):
            for side, row in ((0, yc - 1), (1, 0)):
                base = (row // 8) * 8
                for c in range(0, hw, 512):
                    lo = src[z, :, c:c + 512].astype(F32)[row:row + 1]
                    hi = src[z, :, hw + c:hw + c + 512].astype(F32)[row:row + 1]
                    st[side, z, :, c:c + 512] = jnp.concatenate([lo, hi], axis=0).astype(BF)

    even = 1 - lax.rem(iz, 2)
    s = 2 * even - 1
    pair_plane = (zc - 1) * even
    cross_plane = zc - 1 - pair_plane
    crosses = (iz - s >= 0) & (iz - s < n_z)
    relays = (iz + 2 * s >= 0) & (iz + 2 * s < n_z)

    def ok(dz, dy):
        return has[dz](iz, n_z) & has[dy](iy, n_y)

    def copies(src, st, zb, yb, which):
        found = []
        low, high = pl.ds(0, hw), pl.ds(hw, hw)

        def add(sends, gets, to, src_ref, dst_ref):
            i = len(found)
            found.append((sends, gets, pltpu.make_async_remote_copy(
                src_ref=src_ref, dst_ref=dst_ref,
                send_sem=halo_send.at[which, i], recv_sem=halo_recv.at[which, i],
                device_id=to, device_id_type=MESH)))

        add(None, None, (iz + s, iy), src.at[pair_plane], zb.at[1 - even])
        add(crosses, relays, (iz + s, iy), src.at[cross_plane, :, low], rly.at[which, 0])
        add(crosses, relays, (iz - 2 * s, iy), src.at[cross_plane, :, high], rly.at[which, 1])
        add(relays, crosses, (iz + 2 * s, iy), rly.at[which, 0], zb.at[1 - even, :, low])
        add(relays, crosses, (iz + s, iy), rly.at[which, 1], zb.at[even, :, high])
        for side, dy in ((0, 1), (1, -1)):
            add(ok(0, dy), ok(0, -dy), (iz, iy + dy), st.at[side], yb.at[side, pl.ds(1, zc)])
        for side, dy in ((0, 1), (1, -1)):
            add(ok(1, dy), ok(-1, -dy), (iz + 1, iy + dy), st.at[side, zc - 1], yb.at[side, 0])
            add(ok(-1, dy), ok(1, -dy), (iz - 1, iy + dy), st.at[side, 0], yb.at[side, planes - 1])
        return found

    def guarded(condition, action):
        if condition is None:
            action()
        else:
            pl.when(condition)(action)

    def start(found, picks):
        for i in picks:
            guarded(found[i][0], found[i][2].start)

    def wait_recv(found, picks):
        for i in picks:
            guarded(found[i][1], found[i][2].wait_recv)

    def wait_send(found):
        for sends, _, copy in found:
            guarded(sends, copy.wait_send)

    HOP, PAIR, FORWARD_LOW, FORWARD_HIGH = (1, 2), (0,), (3,), (4,)
    SIDES, CORNERS = (5, 6), (7, 8, 9, 10)

    def clear(zb, yb):
        def one(ref):
            ref[...] = jnp.zeros(ref.shape, BF)

        pl.when(jnp.logical_not(crosses))(lambda: one(zb.at[1 - even]))
        for side, dy in ((0, 1), (1, -1)):
            for dz, ref in ((0, yb.at[side, pl.ds(1, zc)]), (1, yb.at[side, 0]), (-1, yb.at[side, planes - 1])):
                pl.when(jnp.logical_not(ok(-dz, -dy)))(functools.partial(one, ref))

    stage(act, sta)
    clear(za, ya)
    clear(zg, yg)
    diag = sum(ok(dz, dy).astype(jnp.int32) for dz in (-1, 1) for dy in (-1, 1))
    pl.semaphore_wait(barrier, n_y - 1 + n_z - 1 + diag)

    act_copies = copies(act, sta, za, ya, 0)
    start(act_copies, SIDES + HOP + PAIR + CORNERS)

    for load in loads:
        load.wait()

    def gp_step(j, total):
        lanes = pl.ds(pl.multiple_of(j * WIN, WIN), WIN)
        for z in range(zc):
            g = go[z, :, lanes] * mask[z, :, lanes].astype(F32).astype(BF)
            gp[z, :, lanes] = g
            sg[1, j + 1, z + 1] = g
            total = total + jnp.sum(g.astype(F32), axis=0, keepdims=True)
        return total

    bias_total = lax.fori_loop(0, blocks, gp_step, jnp.zeros((1, WIN), F32))
    stage(gp, stg)
    gp_copies = copies(gp, stg, zg, yg, 1)
    wait_recv(act_copies, HOP)
    start(act_copies, FORWARD_LOW + FORWARD_HIGH)
    start(gp_copies, SIDES + HOP + PAIR + CORNERS)

    spread = (iota((ch, WIN), 1) % ch == iota((ch, WIN), 0)).astype(BF)
    k2[...] = jnp.dot(kern[...], spread, preferred_element_type=F32)

    def k2t_step(t, c):
        at = pl.ds(pl.multiple_of(t * ch, ch), ch)
        k2t[at, :] = lax.dot_general(kern[at, :], spread, (((0,), (0,)), ((), ())), preferred_element_type=F32)
        return c

    lax.fori_loop(0, 27, k2t_step, 0)
    lane_vox = iota((ch, WIN), 1) // ch

    def weights(w, t, get):
        blk = [get(e) for e in range(3)]
        for u in range(vox):
            m = jnp.zeros((ch, WIN), F32)
            for e in range(3):
                m = jnp.where(lane_vox == u - e + 1, blk[e], m)
            w[pl.ds(pl.multiple_of(t * WIN + u * ch, ch), ch), :] = m.astype(BF)
        base = taps * WIN
        zero = jnp.zeros((ch, WIN), F32)
        rows_of = [jnp.where(lane_vox == vox - 1, blk[2], zero)] + [zero] * (EDGE // ch - 2) + [jnp.where(lane_vox == 0, blk[0], zero)]
        for r, m in enumerate(rows_of):
            w[pl.ds(pl.multiple_of(base + t * EDGE + r * ch, ch), ch), :] = m.astype(BF)

    def weight_step(t, c):
        weights(wf, t, lambda e: k2[pl.ds(pl.multiple_of((t * 3 + e) * ch, ch), ch), :])
        weights(wb, t, lambda e: k2t[pl.ds(pl.multiple_of(((8 - t) * 3 + 2 - e) * ch, ch), ch), :])
        return c

    lax.fori_loop(0, taps, weight_step, 0)

    per = zc * yc
    for z in range(zc):
        gpt[z] = sg[1, 1:blocks + 1, z + 1].reshape(blocks * yc, WIN).T

    row_id = iota((yc, WIN), 0)
    edge_low = iota((yc, EDGE), 1) < EDGE // 2

    def pad(s):
        for b in range(3):
            s[b, 0] = jnp.zeros((planes, yc, WIN), BF)
            s[b, blocks + 1] = jnp.zeros((planes, yc, WIN), BF)

    def build(local, zb, yb, s, e, which):
        for h in range(2):
            def step(jj, c):
                lanes = pl.ds(pl.multiple_of((h * half + jj) * WIN, WIN), WIN)
                near = pl.ds(pl.multiple_of(jj * WIN, WIN), WIN)
                j = h * half + jj + 1
                for p in which:
                    raw = zb[0, :, lanes] if p == 0 else zb[1, :, lanes] if p == planes - 1 else local[p - 1, :, lanes]
                    x = raw.astype(F32)
                    low = yb[0, p, :, near].astype(F32)[h:h + 1]
                    high = yb[1, p, :, near].astype(F32)[h:h + 1]
                    s[1, j, p] = raw
                    s[0, j, p] = jnp.where(row_id == 0, low, pltpu.roll(x, 1, 0)).astype(BF)
                    s[2, j, p] = jnp.where(row_id == yc - 1, high, pltpu.roll(x, yc - 1, 0)).astype(BF)
                return c
            lax.fori_loop(0, half, step, 0)

        def edges(j, c):
            for b in range(3):
                for p in which:
                    e[b, j, p] = jnp.where(edge_low, s[b, j + 2, p, :, :EDGE], s[b, j, p, :, WIN - EDGE:])
            return c
        lax.fori_loop(0, blocks, edges, 0)

    group = blocks // 3
    m_rows = group * per

    def conv(s, e, w, dst, finish):
        def step(g, c):
            j0 = g * group
            pieces = []
            for a in range(3):
                for b in range(3):
                    pieces.append(s[b, pl.ds(j0 + 1, group), a:a + zc].reshape(m_rows, WIN))
            for a in range(3):
                for b in range(3):
                    pieces.append(e[b, pl.ds(j0, group), a:a + zc].reshape(m_rows, EDGE))
            acc = jnp.dot(jnp.concatenate(pieces, axis=1), w[...], preferred_element_type=F32)
            acc = finish(acc).astype(BF).reshape(group, zc, yc, WIN)
            for q in range(group):
                dst[:, :, pl.ds(pl.multiple_of((j0 + q) * WIN, WIN), WIN)] = acc[q]
            return c
        lax.fori_loop(0, blocks // group, step, 0)

    inner, rim = tuple(range(1, zc + 1)), (0, planes - 1)
    pad(sa)
    pad(sg)
    wait_recv(act_copies, SIDES)
    build(act, za, ya, sa, ea, inner)

    q_vox = iota((WIN, WIN), 0) // ch
    p_vox = iota((WIN, WIN), 1) // ch
    grp = iota((ch, EDGE), 1) // ch

    def fold_lanes(x):
        y = x[:, :EDGE] + x[:, EDGE:] if x.shape[1] == WIN else x
        y = y + pltpu.roll(y, 64, 1)
        return y + pltpu.roll(y, 32, 1)

    def fold_rows(x):
        y = x[:ch]
        for v in range(1, vox):
            y = y + x[v * ch:(v + 1) * ch]
        return y

    def tap(a, b, zs, first):
        t = a * 3 + b
        d, de = None, None
        for z in zs:
            rhs = sa[b, 1:blocks + 1, a + z].reshape(blocks * yc, WIN)
            edge = ea[b, :, a + z].reshape(blocks * yc, EDGE)
            d1 = jnp.dot(gpt[z], rhs, preferred_element_type=F32)
            de1 = jnp.dot(gpt[z], edge, preferred_element_type=F32)
            d, de = (d1, de1) if d is None else (d + d1, de + de1)
        total = jnp.zeros((ch, EDGE), F32)
        for k in range(3):
            one = fold_lanes(fold_rows(jnp.where(p_vox - q_vox + 1 == k, d, 0.0)))
            if k == 0:
                one = one + fold_lanes(jnp.where(grp == EDGE // ch - 1, de[:ch], 0.0))
            if k == 2:
                one = one + fold_lanes(jnp.where(grp == 0, de[WIN - ch:], 0.0))
            total = jnp.where(grp == k, one, total)
        at = pl.ds(pl.multiple_of(t * ch, ch), ch)
        part[at, :] = total if first else part[at, :] + total

    def tap_loop(a, zs, first):
        def step(b, c):
            tap(a, b, zs, first)
            return c
        lax.fori_loop(0, 3, step, 0)

    for a in range(3):
        tap_loop(a, [z for z in range(zc) if a + z in inner], True)
    wait_recv(act_copies, PAIR + FORWARD_LOW + FORWARD_HIGH + CORNERS)
    wait_recv(gp_copies, HOP[1:])
    start(gp_copies, FORWARD_HIGH)
    build(act, za, ya, sa, ea, rim)
    wait_recv(gp_copies, HOP[:1])
    start(gp_copies, FORWARD_LOW)
    for a in (0, 2):
        tap_loop(a, [z for z in range(zc) if a + z in rim], False)
    tail = part.shape[0] - taps * ch
    bias_row = fold_lanes(jnp.broadcast_to(bias_total, (8, WIN)))
    part[taps * ch:taps * ch + 8, :] = bias_row
    if tail > 8:
        part[taps * ch + 8:, :] = jnp.zeros((tail - 8, EDGE), F32)

    a_copies = []
    for k in range(1, n_y):
        to = lax.rem(iy + k, n_y)
        a_copies.append(pltpu.make_async_remote_copy(
            src_ref=part.at[pl.ds(pl.multiple_of(to * rows, 8), rows)], dst_ref=ra.at[k],
            send_sem=a_send.at[k], recv_sem=a_recv.at[k], device_id=(iz, to), device_id_type=MESH))
        a_copies[-1].start()

    bias_row8 = jnp.concatenate([bias[...]] * vox, axis=1)
    conv(sa, ea, wf, out, lambda acc: jnp.maximum(acc + bias_row8, 0.0))

    total = part[pl.ds(pl.multiple_of(iy * rows, 8), rows), :]
    for k, copy in enumerate(a_copies):
        copy.wait_recv()
        total = total + ra[k + 1]
    pa[...] = total
    b_copies = []
    for k in range(1, n_z):
        b_copies.append(pltpu.make_async_remote_copy(
            src_ref=pa, dst_ref=rb.at[iz],
            send_sem=b_send.at[k], recv_sem=b_recv.at[k],
            device_id=(lax.rem(iz + k, n_z), iy), device_id_type=MESH))
        b_copies[-1].start()

    wait_recv(gp_copies, SIDES)
    build(gp, zg, yg, sg, eg, inner)

    rb[pl.ds(iz, 1)] = total[None]
    for copy in b_copies:
        copy.wait_recv()
    total = rb[0]
    for k in range(1, n_z):
        total = total + rb[k]
    pb[...] = total
    mine = pl.ds(pl.multiple_of(iy * rows, 8), rows)
    c_copies = []
    for k in range(1, n_y):
        c_copies.append(pltpu.make_async_remote_copy(
            src_ref=pb, dst_ref=res.at[mine],
            send_sem=c_send.at[k], recv_sem=c_recv.at[k],
            device_id=(iz, lax.rem(iy + k, n_y)), device_id_type=MESH))
        c_copies[-1].start()
    res[mine, :] = total

    wait_recv(gp_copies, PAIR + FORWARD_LOW + FORWARD_HIGH + CORNERS)
    build(gp, zg, yg, sg, eg, rim)
    conv(sg, eg, wb, gin, lambda acc: acc)

    for copy in c_copies:
        copy.wait_recv()
    for t in range(taps):
        turned = (res[t * ch:(t + 1) * ch, :] * scaling).T
        gker[t * 3 * ch:(t + 1) * 3 * ch, :] = turned[:3 * ch]
    gbias[...] = res[taps * ch:taps * ch + 8, :][0:1, :ch] * scaling

    wait_send(act_copies)
    wait_send(gp_copies)
    for copy in a_copies + b_copies + c_copies:
        copy.wait_send()


def local(n_z, n_y, activations, grad_out, relu_mask, kernel, bias):
    zc, yc, width = activations.shape
    ch = kernel.shape[-1]
    blocks = width // WIN
    planes = zc + 2
    voxels = zc * n_z * yc * n_y * (width // ch)
    rows = -(-(9 * ch + 8) // (n_y * 8)) * 8
    cfg = (n_z, n_y, zc, yc, width, ch, rows, 1.0 / math.sqrt(voxels))
    vmem = pl.BlockSpec(memory_space=pltpu.VMEM)
    far = pl.BlockSpec(memory_space=pl.ANY)
    dma = pltpu.SemaphoreType.DMA
    s_shape = pltpu.VMEM((3, blocks + 2, planes, yc, WIN), BF)
    e_shape = pltpu.VMEM((3, blocks, planes, yc, EDGE), BF)
    w_shape = pltpu.VMEM((9 * (WIN + EDGE), WIN), BF)
    k_shape = pltpu.VMEM((27 * ch, WIN), F32)
    stage_shape = pltpu.VMEM((2, zc, 2, width // 2), BF)
    rim_shape = pltpu.VMEM((2, planes, 2, width // 2), BF)
    plane_shape = pltpu.VMEM((2, yc, width), BF)
    output, grad_input, grad_kernel, grad_bias = pl.pallas_call(
        functools.partial(body, cfg),
        out_shape=(
            jax.ShapeDtypeStruct(activations.shape, BF),
            jax.ShapeDtypeStruct(activations.shape, BF),
            jax.ShapeDtypeStruct((27 * ch, ch), F32),
            jax.ShapeDtypeStruct((1, ch), F32),
        ),
        in_specs=[vmem, far, far, vmem, vmem],
        out_specs=(vmem,) * 4,
        scratch_shapes=[
            s_shape, e_shape, s_shape, e_shape, w_shape, w_shape, k_shape, k_shape,
            pltpu.VMEM((zc, yc, width), BF),
            pltpu.VMEM((zc, WIN, blocks * yc), BF),
            plane_shape, plane_shape, stage_shape, stage_shape, rim_shape, rim_shape,
            pltpu.VMEM((n_y * rows, EDGE), F32),
            pltpu.VMEM((n_y, rows, EDGE), F32),
            pltpu.VMEM((rows, EDGE), F32),
            pltpu.VMEM((n_z, rows, EDGE), F32),
            pltpu.VMEM((rows, EDGE), F32),
            pltpu.VMEM((n_y * rows, EDGE), F32),
            pltpu.VMEM((2, 2, yc, width // 2), BF),
            pltpu.VMEM((zc, yc, width), BF), pltpu.VMEM((zc, yc, width), jnp.int32), dma((2,)),
            dma((2, 11)), dma((2, 11)),
            dma((n_y,)), dma((n_y,)), dma((n_z,)), dma((n_z,)), dma((n_y,)), dma((n_y,)),
        ],
        compiler_params=pltpu.CompilerParams(
            collective_id=0, has_side_effects=True, vmem_limit_bytes=60000 * 1024
        ),
    )(activations, grad_out, relu_mask, kernel.reshape(27 * ch, ch), bias.reshape(1, ch))
    return output, grad_input, grad_kernel.reshape(kernel.shape), grad_bias.reshape(ch)


def solution(mesh):
    placed = (P("gz", "gy", None), P("gz", "gy", None), P("gz", "gy", None), P(), P())
    return jax.shard_map(
        functools.partial(local, mesh.shape["gz"], mesh.shape["gy"]),
        mesh=mesh,
        in_specs=placed,
        out_specs=(P("gz", "gy", None), P("gz", "gy", None), P(), P()),
        check_vma=False,
    )
```
